32 devices in a mesh: dir: 2 (over x), shard: 16 (over z, y, core).
Axes of the slice: x: 2, y: 2, z: 4, core: 2. Of those that a mesh axis runs over, the one named last changes fastest.
Arguments:
- propagators: bfloat16 [2, 512, 64, 1024], P('dir', 'shard'), may hold values from 0.5 to 1.5
- field: float32 [64, 1024], replicated, may hold values from -0.5 to 0.5
- orient: float32 [3, 512], replicated, may hold values from -1 to 1, as said below
- quad_weights: float32 [512], replicated, may hold values from 0.01 to 0.1
- analysis: bfloat16 [441, 512], replicated, may hold values from -0.25 to 0.25
- synthesis: bfloat16 [512, 441], replicated, may hold values from -0.4375 to 0.4375
- decay: float32 [441], replicated, may hold values from 0.5 to 1
Outputs:
- density: float32 [64, 1024], P('shard', 'dir')
- qtensor: float32 [5, 64, 1024], P(None, 'shard', 'dir')
The draws below stay inside these ranges and needn't reach their ends.
Inputs may be any that keep to these rules, and one draw needn't show every extreme that they name: Each column of orient is a unit vector.
All inputs are finite; a program needn't handle non-finite values.
Results may differ from the reference program's by a relative error of at most 0.028.
Values may be sent and summed in bfloat16 or wider, within the bound.
A program may use at most 192 MiB of HBM per device.

```python
import math
import jax
import jax.numpy as jnp
from jax import lax

NX = 64
NY = 64
NZ = 16
M = 512
H = 441
STEPS = 2


def draw_orient(key, part):
    polar_key = jax.random.fold_in(key, 11)
    azimuth_key = jax.random.fold_in(key, 12)
    cosine = jax.random.uniform(polar_key, (M,), jnp.float32, -1.0, 1.0)
    azimuth = jax.random.uniform(azimuth_key, (M,), jnp.float32, -math.pi, math.pi)
    sine_polar = jnp.sqrt(jnp.maximum(1.0 - cosine * cosine, 0.0))
    return jnp.stack([sine_polar * jnp.cos(azimuth), sine_polar * jnp.sin(azimuth), cosine])


def block_levels(own_key, extent, split, least, high):
    loudness = 1.0
    for axis_at, blocks in split:
        draws = jax.random.uniform(jax.random.fold_in(jax.random.fold_in(own_key, 6), axis_at), (blocks,), jnp.float32, least / len(split), high / len(split))
        loudness = loudness * jnp.repeat(jnp.exp(draws), extent[axis_at] // blocks).reshape((-1,) + (1,) * (len(extent) - 1 - axis_at))
    return loudness


def gaussian(rng, extent, scale, most, held_as=jnp.bfloat16):
    entries = jax.random.normal(rng, extent, jnp.float32) * scale
    return jnp.minimum(jnp.maximum(entries, -most), most).astype(held_as)


def setup_inputs(seed: int = 0) -> dict:
    key_list = jax.random.split(jax.random.key(seed), 8)
    propagators = jnp.clip(0.5 + 1.0 * jax.random.uniform(key_list[0], (2, M, NX, NY * NZ), jnp.float32) ** block_levels(key_list[0], (2, M, NX, NY * NZ), ((0, 2), (1, 16)), -0.2, 0.2), 0.5, 1.5).astype(jnp.bfloat16)
    field = jnp.clip(jax.random.uniform(key_list[1], (NX, NY * NZ), jnp.float32, -0.5, 0.5), -0.5, 0.5)
    orient = draw_orient(jax.random.fold_in(key_list[7], 71), 0)
    quad_weights = jnp.clip(jnp.exp(jax.random.uniform(key_list[3], (M,), jnp.float32, math.log(0.01), math.log(0.1))), 0.01, 0.1)
    analysis = gaussian(key_list[4], (H, M), M ** -0.5, 0.25)
    synthesis = gaussian(key_list[5], (M, H), (H // 2) ** -0.5, 0.4375)
    decay = jnp.clip(jnp.exp(jax.random.uniform(key_list[6], (H,), jnp.float32, math.log(0.5), math.log(1.0))), 0.5, 1.0)
    return {"propagators": propagators, "field": field, "orient": orient, "quad_weights": quad_weights, "analysis": analysis, "synthesis": synthesis, "decay": decay}


transport_length = 1.5
one_third = 1.0 / 3.0
patterns = {1: "kx,mxyz->mkyz", 2: "ky,mxyz->mxkz", 3: "kz,mxyz->mxyk"}


def dft_tables(length):
    counter = jnp.arange(length, dtype=jnp.int32)
    wrapped = (counter[:, None] * counter[None, :]) % length
    angles = wrapped.astype(jnp.float32) * (2.0 * math.pi / length)
    return jnp.cos(angles).astype(jnp.bfloat16), jnp.sin(angles).astype(jnp.bfloat16)


def wave_numbers(length):
    counter = jnp.arange(length, dtype=jnp.int32)
    signed = jnp.where(counter <= (length - 1) // 2, counter, counter - length)
    return signed.astype(jnp.float32) * (2.0 * math.pi / length)


def phases(heading, direction, lengths):
    wave_x = wave_numbers(lengths[0])[None, :, None, None]
    wave_y = wave_numbers(lengths[1])[None, None, :, None]
    wave_z = wave_numbers(lengths[2])[None, None, None, :]
    phase_angle = (heading[0][:, None, None, None] * wave_x + heading[1][:, None, None, None] * wave_y
                   + heading[2][:, None, None, None] * wave_z) * (direction * transport_length)
    return jnp.cos(phase_angle), jnp.sin(phase_angle)


def along_axis(table, values, position):
    return jnp.einsum(patterns[position], table.astype(jnp.float32), values.astype(jnp.float32))


def complex_pass(tables, real_part, imag_part, position, turning):
    cosine_table, sine_table = tables
    new_real = along_axis(cosine_table, real_part, position) - turning * along_axis(sine_table, imag_part, position)
    new_imag = along_axis(cosine_table, imag_part, position) + turning * along_axis(sine_table, real_part, position)
    return new_real.astype(jnp.bfloat16), new_imag.astype(jnp.bfloat16)


def transport(values, dft_sets, cos_phase, sin_phase, damping):
    cos_x, sin_x = dft_sets[0]
    real_part = along_axis(cos_x, values, 1).astype(jnp.bfloat16)
    imag_part = (-along_axis(sin_x, values, 1)).astype(jnp.bfloat16)
    real_part, imag_part = complex_pass(dft_sets[1], real_part, imag_part, 2, -1.0)
    real_part, imag_part = complex_pass(dft_sets[2], real_part, imag_part, 3, -1.0)
    real_wide = real_part.astype(jnp.float32)
    imag_wide = imag_part.astype(jnp.float32)
    real_part = (real_wide * cos_phase + imag_wide * sin_phase).astype(jnp.bfloat16)
    imag_part = (imag_wide * cos_phase - real_wide * sin_phase).astype(jnp.bfloat16)
    real_part, imag_part = complex_pass(dft_sets[2], real_part, imag_part, 3, 1.0)
    real_part, imag_part = complex_pass(dft_sets[1], real_part, imag_part, 2, 1.0)
    summed = along_axis(cos_x, real_part, 1) - along_axis(sin_x, imag_part, 1)
    return (summed * damping[None]).astype(jnp.bfloat16)


def diffuse(points, analysis, synthesis, decay):
    layout = points.shape
    columns = points.reshape(layout[0], -1)
    harmonic_part = jnp.dot(analysis, columns, preferred_element_type=jnp.float32)
    harmonic_part = (harmonic_part * decay[:, None]).astype(jnp.bfloat16)
    return jnp.dot(synthesis, harmonic_part, preferred_element_type=jnp.float32).astype(jnp.bfloat16).reshape(layout)


def moment_table(orient, quad_weights):
    head_x, head_y, head_z = orient[0], orient[1], orient[2]
    unity = jnp.ones_like(head_x)
    moment_rows = [unity, head_x * head_x - one_third, head_y * head_y - one_third,
                   head_x * head_y, head_x * head_z, head_y * head_z]
    return jnp.stack(moment_rows) * quad_weights[None, :]


def reference(propagators, field, orient, quad_weights, analysis, synthesis, decay):
    propagators = propagators.reshape(2, M, NX, NY, NZ)
    field = field.reshape(NX, NY, NZ)
    dft_sets = [dft_tables(NX), dft_tables(NY), dft_tables(NZ)]
    damping = jnp.exp(-field) / float(NX * NY * NZ)
    block_width = math.gcd(M, 32)
    blocks = M // block_width
    headings = orient.reshape(3, blocks, block_width).transpose(1, 0, 2)

    def advance(state, direction):
        def advance_block(member):
            values, heading = member
            cos_phase, sin_phase = phases(heading, direction, (NX, NY, NZ))
            return transport(values, dft_sets, cos_phase, sin_phase, damping)

        moved = lax.map(advance_block, (state.reshape(blocks, block_width, NX, NY, NZ), headings))
        moved = moved.reshape(M, NX, NY, NZ)
        planes = jnp.moveaxis(moved, 1, 0).reshape(NX, M, NY * NZ)

        def mix_plane(values):
            return diffuse(values, analysis, synthesis, decay)

        diffused = lax.map(mix_plane, planes)
        return jnp.moveaxis(diffused.reshape(NX, M, NY, NZ), 0, 1)

    forward = propagators[0]
    backward = propagators[1]
    for contour in range(STEPS):
        forward = advance(forward, 1.0)
        backward = advance(backward, -1.0)
    product = forward.astype(jnp.float32).reshape(M, -1) * backward.astype(jnp.float32).reshape(M, -1)
    result = jnp.dot(moment_table(orient, quad_weights), product, precision=lax.Precision.HIGHEST)
    return result[0].reshape(NX, NY * NZ), result[1:].reshape(5, NX, NY * NZ)
```

```python
import functools
import math

import jax
import jax.numpy as jnp
import numpy as np
from jax import lax
from jax.experimental import pallas as pl
from jax.experimental.pallas import tpu as pltpu
from jax.sharding import PartitionSpec as P

NY = 64
STEPS = 2

transport_length = 1.5
one_third = 1.0 / 3.0
VMEM_LIMIT = 60 * 1024 * 1024


def half_spectrum(ny, nz):
    selfs = [(0, 0), (ny // 2, 0), (0, nz // 2), (ny // 2, nz // 2)]
    pairs = []
    for ky in range(ny):
        for kz in range(nz):
            mirror = ((-ky) % ny, (-kz) % nz)
            if (ky, kz) < mirror:
                pairs.append((ky, kz))
    first = selfs[:2] + pairs
    second = selfs[2:] + pairs
    return np.array(first + second, np.int64)


def real_basis(ny, nz):
    freq = half_spectrum(ny, nz)
    half = len(freq) // 2
    y = np.repeat(np.arange(ny), nz)[:, None]
    z = np.tile(np.arange(nz), ny)[:, None]
    angle = 2.0 * np.pi * (y * freq[None, :, 0] / ny + z * freq[None, :, 1] / nz)
    basis = np.cos(angle)
    basis[:, half + 2 :] = -np.sin(angle[:, half + 2 :])
    return basis


def signed(k, length):
    return np.where(k <= (length - 1) // 2, k, k - length) * (2.0 * np.pi / length)


def plane_tables(heading, scale, ny, nz):
    freq = half_spectrum(ny, nz)
    lanes = len(freq)
    half = lanes // 2
    wave_y = jnp.asarray(signed(freq[:, 0], ny), jnp.float32)
    wave_z = jnp.asarray(signed(freq[:, 1], nz), jnp.float32)
    theta_y = scale * heading[1][:, None] * wave_y[None, :]
    theta_z = scale * heading[2][:, None] * wave_z[None, :]
    cy, sy, cz, sz = jnp.cos(theta_y), jnp.sin(theta_y), jnp.cos(theta_z), jnp.sin(theta_z)
    ny_mask = freq[:, 0] == ny // 2
    nz_mask = freq[:, 1] == nz // 2
    only_y = jnp.asarray(ny_mask & ~nz_mask)[None]
    only_z = jnp.asarray(nz_mask & ~ny_mask)[None]
    both = jnp.asarray(ny_mask & nz_mask)[None]
    cos_sum = cy * cz - sy * sz
    sin_sum = sy * cz + cy * sz
    single = only_y | only_z
    cu = jnp.where(single, cy * cz, cos_sum)
    su = jnp.where(only_z, sy * cz, jnp.where(only_y, sz * cy, jnp.where(both, 0.0, sin_sum)))
    cv = jnp.where(
        only_z, -cy * sz, jnp.where(only_y, -cz * sy, jnp.where(both, -sin_sum, 0.0))
    )
    sv = jnp.where(single, -sy * sz, 0.0)
    weight = np.full((lanes,), 2.0 / (ny * nz))
    weight[[0, 1, half, half + 1]] = 1.0 / (ny * nz)
    turn = np.where(np.arange(lanes) < half, 1.0, -1.0)
    weight = jnp.asarray(weight, jnp.float32)[None]
    turn = jnp.asarray(turn, jnp.float32)[None]
    return cu * weight, su * weight * turn, cv * weight, sv * weight * turn


def line_operator(heading, scale, nx, group):
    count = heading.shape[1]
    k = np.arange(1, nx // 2)
    theta = scale * heading[0][:, None] * jnp.asarray(k * (2.0 * np.pi / nx), jnp.float32)[None]
    theta_n = -scale * heading[0][:, None] * math.pi
    trig = jnp.concatenate(
        [jnp.ones((count, 1), jnp.float32), jnp.cos(theta), jnp.sin(theta), jnp.cos(theta_n)], 1
    )
    gap = (np.arange(nx)[:, None] - np.arange(nx)[None, :]) % nx
    angle = 2.0 * np.pi * ((k[:, None, None] * gap[None]) % nx) / nx
    rows = np.concatenate(
        [np.ones((1, nx, nx)), 2 * np.cos(angle), 2 * np.sin(angle), (1.0 - 2.0 * (gap % 2))[None]]
    )
    table = jnp.asarray(rows / nx, jnp.float32)
    operator = jnp.einsum("gmk,kax->gamx", trig.reshape(-1, group, nx), table,
                          precision=lax.Precision.HIGHEST)
    operator = operator.reshape(count // group, nx * group, nx)
    sign = jnp.asarray(1.0 - 2.0 * (np.arange(nx) % 2), jnp.float32)
    extra = jnp.broadcast_to(sign, (count // group, group, nx))
    operator = jnp.concatenate([operator, extra], 1).astype(jnp.bfloat16)
    return operator, jnp.sin(theta_n) / nx


def to_rows(block):
    a, b, lanes = block.shape
    if b % 16:
        return block.astype(jnp.float32).reshape(a * b, lanes).astype(jnp.bfloat16)
    return block.reshape(a * b, lanes)


def swap(values):
    half = values.shape[-1] // 2
    return jnp.concatenate([values[..., half:], values[..., :half]], axis=-1)


def transport_kernel(by_cell, group, nx, halves, q_ref, p_ref, c_ref, s_ref, cv_ref, sv_ref,
                     w_ref, damping_ref, out_ref, z_ref, l_ref):
    rows = nx * group
    lanes = w_ref.shape[1]
    width = lanes // halves
    col = lax.broadcasted_iota(jnp.int32, (nx, rows), 1)
    line = lax.broadcasted_iota(jnp.int32, (nx, rows), 0)
    col_x = col // group if by_cell else col % nx
    expand = jnp.where(col_x == line, 1.0, 0.0).astype(jnp.bfloat16)
    wide = jnp.dot(p_ref[0], expand, preferred_element_type=jnp.float32)
    row_at = lax.broadcasted_iota(jnp.int32, wide.shape, 0)
    col_at = lax.broadcasted_iota(jnp.int32, wide.shape, 1)
    col_m = col_at % group if by_cell else col_at // nx
    l_ref[...] = jnp.where(row_at % group == col_m, wide, 0.0).astype(jnp.bfloat16)

    outer = q_ref.shape[0]
    chunks = 4
    part = outer // chunks
    step_rows = rows // chunks

    def forward(i, carry):
        block = to_rows(q_ref[pl.ds(i * part, part)])
        z = jnp.dot(block, w_ref[...], preferred_element_type=jnp.float32)
        start = pl.multiple_of(i * step_rows, step_rows)
        z_ref[pl.ds(start, step_rows), :] = z.astype(jnp.bfloat16)
        return carry

    lax.fori_loop(0, chunks, forward, 0)

    ripple = jnp.dot(l_ref[rows:, :], z_ref[...], preferred_element_type=jnp.float32)
    cross = ripple * cv_ref[...] + swap(ripple) * sv_ref[...]
    part_x = nx // chunks

    def backward(i, carry):
        start = pl.multiple_of(i * step_rows, step_rows)
        y = jnp.dot(l_ref[pl.ds(start, step_rows), :], z_ref[...],
                    preferred_element_type=jnp.float32)
        y = y.reshape(part_x, group, lanes)
        odd = lax.broadcasted_iota(jnp.int32, y.shape, 0) % 2 == 1
        turned = y * c_ref[...][None] + swap(y) * s_ref[...][None]
        turned = turned + jnp.where(odd, -cross[None], cross[None])
        turned = turned.reshape(step_rows, lanes).astype(jnp.bfloat16)
        back = lax.dot_general(turned, w_ref[...], (((1,), (1,)), ((), ())),
                               preferred_element_type=jnp.float32)
        x_at = pl.multiple_of(i * part_x, part_x)
        back = back.reshape(part_x, group, lanes) * damping_ref[pl.ds(x_at, part_x), :][:, None, :]
        back = back.astype(jnp.bfloat16)
        for h in range(halves):
            out_ref[h, pl.ds(x_at, part_x)] = back[:, :, h * width : (h + 1) * width]
        return carry

    lax.fori_loop(0, chunks, backward, 0)


def transport(q, by_cell, halves, operator, tables, basis, damping):
    nx, lanes = damping.shape
    count = q.shape[1] if by_cell else q.shape[0]
    group = operator.shape[1] // (nx + 1)
    rows = nx * group


    if by_cell:
        q_spec = pl.BlockSpec((nx, group, lanes), lambda g: (0, g, 0))
    else:
        q_spec = pl.BlockSpec((group, nx, lanes), lambda g: (g, 0, 0))
    table_spec = pl.BlockSpec((group, lanes), lambda g: (g, 0))
    return pl.pallas_call(
        functools.partial(transport_kernel, by_cell, group, nx, halves),
        out_shape=jax.ShapeDtypeStruct((halves, nx, count, lanes // halves), jnp.bfloat16),
        grid=(count // group,),
        in_specs=[
            q_spec,
            pl.BlockSpec((1, rows + group, nx), lambda g: (g, 0, 0)),
            table_spec, table_spec, table_spec, table_spec,
            pl.BlockSpec((lanes, lanes), lambda g: (0, 0)),
            pl.BlockSpec((nx, lanes), lambda g: (0, 0)),
        ],
        out_specs=pl.BlockSpec((halves, nx, group, lanes // halves), lambda g: (0, 0, g, 0)),
        scratch_shapes=[
            pltpu.VMEM((rows, lanes), jnp.bfloat16),
            pltpu.VMEM((rows + group, rows), jnp.bfloat16),
        ],
        compiler_params=pltpu.CompilerParams(vmem_limit_bytes=VMEM_LIMIT),
    )(q, operator, *tables, basis, damping)


def mix(block, analysis_ref, synthesis_ref, decay_ref):
    harmonic = jnp.dot(analysis_ref[...], block, preferred_element_type=jnp.float32)
    harmonic = (harmonic * decay_ref[...]).astype(jnp.bfloat16)
    return jnp.dot(synthesis_ref[...], harmonic, preferred_element_type=jnp.float32)


def diffuse_kernel(points_ref, analysis_ref, synthesis_ref, decay_ref, out_ref):
    n, _, count, width = points_ref.shape
    block = to_rows(points_ref[:, 0])
    mixed = mix(block, analysis_ref, synthesis_ref, decay_ref)
    out_ref[:, 0] = mixed.reshape(n, count, width).astype(jnp.bfloat16)


def diffuse(points, analysis, synthesis, decay):
    n, rows, count, lanes = points.shape
    width = lanes // 2
    spec = pl.BlockSpec((n, 1, count, width), lambda i, j: (0, i, 0, j))
    whole = pl.BlockSpec(analysis.shape, lambda i, j: (0, 0))
    return pl.pallas_call(
        diffuse_kernel,
        out_shape=jax.ShapeDtypeStruct(points.shape, jnp.bfloat16),
        grid=(rows, 2),
        in_specs=[
            spec,
            whole,
            pl.BlockSpec(synthesis.shape, lambda i, j: (0, 0)),
            pl.BlockSpec(decay.shape, lambda i, j: (0, 0)),
        ],
        out_specs=spec,
        compiler_params=pltpu.CompilerParams(vmem_limit_bytes=VMEM_LIMIT),
    )(points, analysis, synthesis, decay)


def moment_kernel(points_ref, analysis_ref, synthesis_ref, decay_ref, table_ref, out_ref):
    product = None
    for p in range(2):
        block = to_rows(points_ref[p, :, 0])
        mixed = mix(block, analysis_ref, synthesis_ref, decay_ref)
        mixed = mixed.astype(jnp.bfloat16).astype(jnp.float32)
        product = mixed if product is None else product * mixed
    out_ref[0] = jnp.dot(table_ref[...], product, precision=lax.Precision.HIGHEST,
                         preferred_element_type=jnp.float32)


def moments(points, analysis, synthesis, decay, table):
    two, n, rows, count, width = points.shape
    return pl.pallas_call(
        moment_kernel,
        out_shape=jax.ShapeDtypeStruct((rows, table.shape[0], width), jnp.float32),
        grid=(rows,),
        in_specs=[
            pl.BlockSpec((two, n, 1, count, width), lambda i: (0, 0, i, 0, 0)),
            pl.BlockSpec(analysis.shape, lambda i: (0, 0)),
            pl.BlockSpec(synthesis.shape, lambda i: (0, 0)),
            pl.BlockSpec(decay.shape, lambda i: (0, 0)),
            pl.BlockSpec(table.shape, lambda i: (0, 0)),
        ],
        out_specs=pl.BlockSpec((1, table.shape[0], width), lambda i: (i, 0, 0)),
        compiler_params=pltpu.CompilerParams(vmem_limit_bytes=VMEM_LIMIT),
    )(points, analysis, synthesis, decay, table)


def moment_table(orient, quad_weights):
    head_x, head_y, head_z = (orient[0], orient[1], orient[2])
    unity = jnp.ones_like(head_x)
    zero = jnp.zeros_like(head_x)
    moment_rows = [
        unity,
        head_x * head_x - one_third,
        head_y * head_y - one_third,
        head_x * head_y,
        head_x * head_z,
        head_y * head_z,
        zero,
        zero,
    ]
    return jnp.stack(moment_rows) * quad_weights[None, :]


def on_device(propagators, field, orient, quad_weights, analysis, synthesis, decay):
    state = propagators[0]
    count, nx, lanes = state.shape
    nz = lanes // NY
    shards = lax.axis_size("shard")
    group = min(16, count)
    offset = lax.axis_index("shard") * count
    heading = lax.dynamic_slice_in_dim(orient, offset, count, 1)
    direction = 1.0 - 2.0 * lax.axis_index("dir").astype(jnp.float32)
    scale = direction * transport_length
    operator, nyquist = line_operator(heading, scale, nx, group)
    cu, su, cv, sv = plane_tables(heading, scale, NY, nz)
    tables = (cu, su, cv * nyquist, sv * nyquist)
    basis = jnp.asarray(real_basis(NY, nz).astype(jnp.bfloat16))
    damping = jnp.exp(-field)
    harmonics, total = analysis.shape
    pad = -harmonics % 128
    analysis = jnp.pad(analysis, ((0, pad), (0, 0)))
    synthesis = jnp.pad(synthesis, ((0, 0), (0, pad)))
    decay = jnp.pad(decay, (0, pad))[:, None]

    by_cell = False
    for contour in range(STEPS):
        is_last = contour == STEPS - 1
        halves = lax.axis_size("dir") if is_last else 1
        moved = transport(state, by_cell, halves, operator, tables, basis, damping)
        if is_last:
            moved = moved.reshape(halves * shards, nx // shards, count, lanes // halves)
            moved = lax.all_to_all(moved, ("dir", "shard"), 0, 0, tiled=True)
            moved = moved.reshape(halves, shards, nx // shards, count, lanes // halves)
            table = moment_table(orient, quad_weights)
            result = moments(moved, analysis, synthesis, decay, table)
        else:
            moved = moved.reshape(shards, nx // shards, count, lanes)
            moved = lax.all_to_all(moved, "shard", 0, 0, tiled=True)
            mixed = diffuse(moved, analysis, synthesis, decay)
            mixed = lax.all_to_all(mixed, "shard", 0, 0, tiled=True)
            state = mixed.reshape(nx, count, lanes)
            by_cell = True
    return result[:, 0], jnp.moveaxis(result[:, 1:6], 1, 0)


def solution(mesh):
    in_specs = (P("dir", "shard", None, None), P(), P(), P(), P(), P(), P())
    out_specs = (P("shard", "dir"), P(None, "shard", "dir"))
    return jax.shard_map(
        on_device, mesh=mesh, in_specs=in_specs, out_specs=out_specs, check_vma=False
    )
```

```python
import functools
import math

import jax
import jax.numpy as jnp
import numpy as np
from jax import lax
from jax.experimental import pallas as pl
from jax.experimental.pallas import tpu as pltpu
from jax.sharding import PartitionSpec as P

NY = 64
STEPS = 2

transport_length = 1.5
one_third = 1.0 / 3.0
VMEM_LIMIT = 60 * 1024 * 1024
MESH = pl.DeviceIdType.MESH
CUBE = False


def half_spectrum(ny, nz):
    selfs = [(0, 0), (ny // 2, 0), (0, nz // 2), (ny // 2, nz // 2)]
    pairs = []
    for ky in range(ny):
        for kz in range(nz):
            mirror = ((-ky) % ny, (-kz) % nz)
            if (ky, kz) < mirror:
                pairs.append((ky, kz))
    first = selfs[:2] + pairs
    second = selfs[2:] + pairs
    return np.array(first + second, np.int64)


def real_basis(ny, nz):
    freq = half_spectrum(ny, nz)
    half = len(freq) // 2
    y = np.repeat(np.arange(ny), nz)[:, None]
    z = np.tile(np.arange(nz), ny)[:, None]
    angle = 2.0 * np.pi * (y * freq[None, :, 0] / ny + z * freq[None, :, 1] / nz)
    basis = np.cos(angle)
    basis[:, half + 2 :] = -np.sin(angle[:, half + 2 :])
    return basis


def signed(k, length):
    return np.where(k <= (length - 1) // 2, k, k - length) * (2.0 * np.pi / length)


def plane_tables(heading, scale, ny, nz):
    freq = half_spectrum(ny, nz)
    lanes = len(freq)
    half = lanes // 2
    wave_y = jnp.asarray(signed(freq[:, 0], ny), jnp.float32)
    wave_z = jnp.asarray(signed(freq[:, 1], nz), jnp.float32)
    theta_y = scale * heading[1][:, None] * wave_y[None, :]
    theta_z = scale * heading[2][:, None] * wave_z[None, :]
    cy, sy, cz, sz = jnp.cos(theta_y), jnp.sin(theta_y), jnp.cos(theta_z), jnp.sin(theta_z)
    ny_mask = freq[:, 0] == ny // 2
    nz_mask = freq[:, 1] == nz // 2
    only_y = jnp.asarray(ny_mask & ~nz_mask)[None]
    only_z = jnp.asarray(nz_mask & ~ny_mask)[None]
    both = jnp.asarray(ny_mask & nz_mask)[None]
    cos_sum = cy * cz - sy * sz
    sin_sum = sy * cz + cy * sz
    single = only_y | only_z
    cu = jnp.where(single, cy * cz, cos_sum)
    su = jnp.where(only_z, sy * cz, jnp.where(only_y, sz * cy, jnp.where(both, 0.0, sin_sum)))
    cv = jnp.where(
        only_z, -cy * sz, jnp.where(only_y, -cz * sy, jnp.where(both, -sin_sum, 0.0))
    )
    sv = jnp.where(single, -sy * sz, 0.0)
    weight = np.full((lanes,), 2.0 / (ny * nz))
    weight[[0, 1, half, half + 1]] = 1.0 / (ny * nz)
    turn = np.where(np.arange(lanes) < half, 1.0, -1.0)
    weight = jnp.asarray(weight, jnp.float32)[None]
    turn = jnp.asarray(turn, jnp.float32)[None]
    return cu * weight, su * weight * turn, cv * weight, sv * weight * turn


def line_operator(heading, scale, nx, group):
    count = heading.shape[1]
    k = np.arange(1, nx // 2)
    theta = scale * heading[0][:, None] * jnp.asarray(k * (2.0 * np.pi / nx), jnp.float32)[None]
    theta_n = -scale * heading[0][:, None] * math.pi
    trig = jnp.concatenate(
        [jnp.ones((count, 1), jnp.float32), jnp.cos(theta), jnp.sin(theta), jnp.cos(theta_n)], 1
    )
    gap = (np.arange(nx)[:, None] - np.arange(nx)[None, :]) % nx
    angle = 2.0 * np.pi * ((k[:, None, None] * gap[None]) % nx) / nx
    rows = np.concatenate(
        [np.ones((1, nx, nx)), 2 * np.cos(angle), 2 * np.sin(angle), (1.0 - 2.0 * (gap % 2))[None]]
    )
    table = jnp.asarray(rows / nx, jnp.float32)
    operator = jnp.einsum("gmk,kax->gamx", trig.reshape(-1, group, nx), table,
                          precision=lax.Precision.HIGHEST)
    operator = operator.reshape(count // group, nx * group, nx)
    sign = jnp.asarray(1.0 - 2.0 * (np.arange(nx) % 2), jnp.float32)
    extra = jnp.broadcast_to(sign, (count // group, group, nx))
    operator = jnp.concatenate([operator, extra], 1).astype(jnp.bfloat16)
    return operator, jnp.sin(theta_n) / nx


def to_rows(block):
    a, b, lanes = block.shape
    if b % 16:
        return block.astype(jnp.float32).reshape(a * b, lanes).astype(jnp.bfloat16)
    return block.reshape(a * b, lanes)


def swap(values):
    half = values.shape[-1] // 2
    return jnp.concatenate([values[..., half:], values[..., :half]], axis=-1)


def my_place(cube):
    d, s, n = lax.axis_index("dir"), lax.axis_index("shard"), lax.axis_size("shard")
    if not cube:
        return d, s
    half = n // 2
    return s // half, d * half + s % half


def place(cube, p, block):
    if not cube:
        return p, block
    half = lax.axis_size("shard") // 2
    return block // half, p * half + block % half


def greet():
    d, s = lax.axis_index("dir"), lax.axis_index("shard")
    two, n = lax.axis_size("dir"), lax.axis_size("shard")
    barrier = pltpu.get_barrier_semaphore()

    def one(k, carry):
        other = (d * n + s + k) % (two * n)
        pl.semaphore_signal(barrier, inc=1, device_id=(other // n, other % n), device_id_type=MESH)
        return carry

    lax.fori_loop(1, two * n, one, 0)


def greeted():
    others = lax.axis_size("dir") * lax.axis_size("shard") - 1
    pl.semaphore_wait(pltpu.get_barrier_semaphore(), others)


def remote(source, target, send, receive, device):
    return pltpu.make_async_remote_copy(
        src_ref=source, dst_ref=target, send_sem=send, recv_sem=receive,
        device_id=device, device_id_type=MESH,
    )


def is_me(device):
    return (device[0] == lax.axis_index("dir")) & (device[1] == lax.axis_index("shard"))


def transport_kernel(cube, by_cell, group, nx, halves, q_ref, p_ref, c_ref, s_ref, cv_ref, sv_ref,
                     w_ref, damping_ref, out_ref, z_ref, l_ref, stage_ref, send_sem, recv_sem,
                     local_sem):
    greet()
    rows = nx * group
    lanes = w_ref.shape[1]
    width = lanes // halves
    groups = p_ref.shape[0]
    n = lax.axis_size("shard")
    slab = nx // n
    here = (lax.axis_index("dir"), lax.axis_index("shard"))
    held_p, held_block = my_place(cube and by_cell)
    new_p, _ = my_place(cube)
    slot_me = held_p * n + held_block if halves > 1 else held_block

    def target(h, t):
        return (h, t) if halves > 1 else place(cube, held_p, t)

    def origin(slot):
        if halves > 1:
            return place(cube, slot // n, slot % n)
        return new_p, slot

    def copy_out(g, h, t):
        device = target(h, t)
        return remote(
            stage_ref.at[h, g, pl.ds(t * slab, slab)],
            out_ref.at[slot_me, :, pl.ds(pl.multiple_of(g * group, group), group), :],
            send_sem.at[g, h * n + t], recv_sem.at[g, slot_me], device,
        )

    def copy_here(g, h, t):
        return pltpu.make_async_copy(
            stage_ref.at[h, g, pl.ds(t * slab, slab)],
            out_ref.at[slot_me, :, pl.ds(pl.multiple_of(g * group, group), group), :],
            local_sem.at[g],
        )

    col = lax.broadcasted_iota(jnp.int32, (nx, rows), 1)
    line = lax.broadcasted_iota(jnp.int32, (nx, rows), 0)
    col_x = col // group if by_cell else col % nx
    expand = jnp.where(col_x == line, 1.0, 0.0).astype(jnp.bfloat16)

    chunks = 4
    outer = nx if by_cell else group
    part = outer // chunks
    step_rows = rows // chunks
    part_x = nx // chunks
    per = n // chunks
    first = held_block // per + chunks // 2

    def one_group(g, carry):
        wide = jnp.dot(p_ref[g], expand, preferred_element_type=jnp.float32)
        row_at = lax.broadcasted_iota(jnp.int32, wide.shape, 0)
        col_at = lax.broadcasted_iota(jnp.int32, wide.shape, 1)
        col_m = col_at % group if by_cell else col_at // nx
        l_ref[...] = jnp.where(row_at % group == col_m, wide, 0.0).astype(jnp.bfloat16)
        m_at = pl.ds(pl.multiple_of(g * group, group), group)

        def forward(i, carry):
            if by_cell:
                block = to_rows(q_ref[pl.ds(i * part, part), m_at, :])
            else:
                block = to_rows(q_ref[pl.ds(g * group + i * part, part)])
            z = jnp.dot(block, w_ref[...], preferred_element_type=jnp.float32)
            start = pl.multiple_of(i * step_rows, step_rows)
            z_ref[pl.ds(start, step_rows), :] = z.astype(jnp.bfloat16)
            return carry

        lax.fori_loop(0, chunks, forward, 0)

        ripple = jnp.dot(l_ref[rows:, :], z_ref[...], preferred_element_type=jnp.float32)
        cross = ripple * cv_ref[m_at, :] + swap(ripple) * sv_ref[m_at, :]

        @pl.when(g == 0)
        def _():
            greeted()

        def backward(j, carry):
            i = (first + j) % chunks
            start = pl.multiple_of(i * step_rows, step_rows)
            y = jnp.dot(l_ref[pl.ds(start, step_rows), :], z_ref[...],
                        preferred_element_type=jnp.float32)
            y = y.reshape(part_x, group, lanes)
            odd = lax.broadcasted_iota(jnp.int32, y.shape, 0) % 2 == 1
            turned = y * c_ref[m_at, :][None] + swap(y) * s_ref[m_at, :][None]
            turned = turned + jnp.where(odd, -cross[None], cross[None])
            turned = turned.reshape(step_rows, lanes).astype(jnp.bfloat16)
            back = lax.dot_general(turned, w_ref[...], (((1,), (1,)), ((), ())),
                                   preferred_element_type=jnp.float32)
            x_at = pl.ds(pl.multiple_of(i * part_x, part_x), part_x)
            back = back.reshape(part_x, group, lanes) * damping_ref[x_at, :][:, None, :]
            back = back.astype(jnp.bfloat16)
            for h in range(halves):
                stage_ref[h, g, x_at] = back[:, :, h * width : (h + 1) * width]

            def send(k, carry):
                t = i * per + (held_block + k) % per
                for h in range(halves):
                    mine = is_me(target(h, t))

                    @pl.when(mine)
                    def _():
                        copy_here(g, h, t).start()

                    @pl.when(jnp.logical_not(mine))
                    def _():
                        copy_out(g, h, t).start()
                return carry

            lax.fori_loop(0, per, send, 0)
            return carry

        lax.fori_loop(0, chunks, backward, 0)
        return carry

    lax.fori_loop(0, groups, one_group, 0)

    def finish(g, carry):
        def sent(t, carry):
            for h in range(halves):
                mine = is_me(target(h, t))

                @pl.when(mine)
                def _():
                    copy_here(g, h, t).wait()

                @pl.when(jnp.logical_not(mine))
                def _():
                    copy_out(g, h, t).wait_send()
            return carry

        lax.fori_loop(0, n, sent, 0)

        def received(slot, carry):
            @pl.when(jnp.logical_not(is_me(origin(slot))))
            def _():
                remote(
                    stage_ref.at[0, g, pl.ds(0, slab)],
                    out_ref.at[slot, :, pl.ds(pl.multiple_of(g * group, group), group), :],
                    send_sem.at[g, slot], recv_sem.at[g, slot], here,
                ).wait_recv()
            return carry

        lax.fori_loop(0, halves * n, received, 0)
        return carry

    lax.fori_loop(0, groups, finish, 0)


def transport(cube, q, by_cell, halves, operator, tables, basis, damping):
    nx, lanes = damping.shape
    count = q.shape[1] if by_cell else q.shape[0]
    group = operator.shape[1] // (nx + 1)
    rows = nx * group
    groups = count // group
    n = lax.axis_size("shard")
    width = lanes // halves
    vmem = pl.BlockSpec(memory_space=pltpu.VMEM)
    return pl.pallas_call(
        functools.partial(transport_kernel, cube, by_cell, group, nx, halves),
        out_shape=jax.ShapeDtypeStruct((halves * n, nx // n, count, width), jnp.bfloat16),
        in_specs=[vmem] * 8,
        out_specs=pl.BlockSpec(memory_space=pl.ANY),
        scratch_shapes=[
            pltpu.VMEM((rows, lanes), jnp.bfloat16),
            pltpu.VMEM((rows + group, rows), jnp.bfloat16),
            pltpu.VMEM((halves, groups, nx, group, width), jnp.bfloat16),
            pltpu.SemaphoreType.DMA((groups, halves * n)),
            pltpu.SemaphoreType.DMA((groups, halves * n)),
            pltpu.SemaphoreType.DMA((groups,)),
        ],
        compiler_params=pltpu.CompilerParams(
            vmem_limit_bytes=VMEM_LIMIT, collective_id=2 if by_cell else 0, has_side_effects=True
        ),
    )(q, operator, *tables, basis, damping)


def mix(block, analysis_ref, synthesis_ref, decay_ref):
    harmonic = jnp.dot(analysis_ref[...], block, preferred_element_type=jnp.float32)
    harmonic = (harmonic * decay_ref[...]).astype(jnp.bfloat16)
    return jnp.dot(synthesis_ref[...], harmonic, preferred_element_type=jnp.float32)


def diffuse_kernel(cube, points_ref, analysis_ref, synthesis_ref, decay_ref, out_ref, stage_ref,
                   send_sem, recv_sem, local_sem):
    greet()
    n, slab, count, lanes = points_ref.shape
    here = (lax.axis_index("dir"), lax.axis_index("shard"))
    p, me = my_place(cube)
    width = lanes // 2

    def copy_out(i, t):
        return remote(stage_ref.at[t, i], out_ref.at[me * slab + i], send_sem.at[i, t],
                      recv_sem.at[i, me], place(cube, p, t))

    def copy_here(i):
        return pltpu.make_async_copy(stage_ref.at[me, i], out_ref.at[me * slab + i],
                                     local_sem.at[i])

    def one_row(i, carry):
        for j in range(2):
            at = slice(j * width, (j + 1) * width)
            block = to_rows(points_ref[:, i, :, at])
            mixed = mix(block, analysis_ref, synthesis_ref, decay_ref)
            stage_ref[:, i, :, at] = mixed.reshape(n, count, width).astype(jnp.bfloat16)

        @pl.when(i == 0)
        def _():
            greeted()

        def send(k, carry):
            copy_out(i, (me + n // 2 + k) % n).start()
            return carry

        lax.fori_loop(0, n // 2, send, 0)
        lax.fori_loop(n // 2 + 1, n, send, 0)
        copy_here(i).start()
        return carry

    lax.fori_loop(0, slab, one_row, 0)

    def finish(i, carry):
        def one(k, carry):
            t = (me + k) % n
            copy_out(i, t).wait_send()
            remote(stage_ref.at[t, i], out_ref.at[t * slab + i], send_sem.at[i, t],
                   recv_sem.at[i, t], here).wait_recv()
            return carry

        lax.fori_loop(1, n, one, 0)
        copy_here(i).wait()
        return carry

    lax.fori_loop(0, slab, finish, 0)


def diffuse(cube, points, analysis, synthesis, decay):
    n, slab, count, lanes = points.shape
    vmem = pl.BlockSpec(memory_space=pltpu.VMEM)
    return pl.pallas_call(
        functools.partial(diffuse_kernel, cube),
        out_shape=jax.ShapeDtypeStruct((n * slab, count, lanes), jnp.bfloat16),
        in_specs=[vmem] * 4,
        out_specs=pl.BlockSpec(memory_space=pl.ANY),
        scratch_shapes=[
            pltpu.VMEM(points.shape, jnp.bfloat16),
            pltpu.SemaphoreType.DMA((slab, n)),
            pltpu.SemaphoreType.DMA((slab, n)),
            pltpu.SemaphoreType.DMA((slab,)),
        ],
        compiler_params=pltpu.CompilerParams(
            vmem_limit_bytes=VMEM_LIMIT, collective_id=1, has_side_effects=True
        ),
    )(points, analysis, synthesis, decay)


def moment_kernel(points_ref, analysis_ref, synthesis_ref, decay_ref, table_ref, out_ref):
    product = None
    for p in range(2):
        block = to_rows(points_ref[p, :, 0])
        mixed = mix(block, analysis_ref, synthesis_ref, decay_ref)
        mixed = mixed.astype(jnp.bfloat16).astype(jnp.float32)
        product = mixed if product is None else product * mixed
    out_ref[0] = jnp.dot(table_ref[...], product, precision=lax.Precision.HIGHEST,
                         preferred_element_type=jnp.float32)


def moments(points, analysis, synthesis, decay, table):
    two, n, rows, count, width = points.shape
    return pl.pallas_call(
        moment_kernel,
        out_shape=jax.ShapeDtypeStruct((rows, table.shape[0], width), jnp.float32),
        grid=(rows,),
        in_specs=[
            pl.BlockSpec((two, n, 1, count, width), lambda i: (0, 0, i, 0, 0)),
            pl.BlockSpec(analysis.shape, lambda i: (0, 0)),
            pl.BlockSpec(synthesis.shape, lambda i: (0, 0)),
            pl.BlockSpec(decay.shape, lambda i: (0, 0)),
            pl.BlockSpec(table.shape, lambda i: (0, 0)),
        ],
        out_specs=pl.BlockSpec((1, table.shape[0], width), lambda i: (i, 0, 0)),
        compiler_params=pltpu.CompilerParams(vmem_limit_bytes=VMEM_LIMIT),
    )(points, analysis, synthesis, decay, table)


def moment_table(orient, quad_weights):
    head_x, head_y, head_z = (orient[0], orient[1], orient[2])
    unity = jnp.ones_like(head_x)
    zero = jnp.zeros_like(head_x)
    moment_rows = [
        unity,
        head_x * head_x - one_third,
        head_y * head_y - one_third,
        head_x * head_y,
        head_x * head_z,
        head_y * head_z,
        zero,
        zero,
    ]
    return jnp.stack(moment_rows) * quad_weights[None, :]


def on_device(propagators, field, orient, quad_weights, analysis, synthesis, decay):
    state = propagators[0]
    count, nx, lanes = state.shape
    nz = lanes // NY
    group = min(16, count)
    basis = jnp.asarray(real_basis(NY, nz).astype(jnp.bfloat16))
    damping = jnp.exp(-field)
    harmonics, total = analysis.shape
    pad = -harmonics % 128
    analysis = jnp.pad(analysis, ((0, pad), (0, 0)))
    synthesis = jnp.pad(synthesis, ((0, 0), (0, pad)))
    decay = jnp.pad(decay, (0, pad))[:, None]

    def held(p, block):
        heading = lax.dynamic_slice_in_dim(orient, block * count, count, 1)
        scale = (1.0 - 2.0 * p.astype(jnp.float32)) * transport_length
        operator, nyquist = line_operator(heading, scale, nx, group)
        cu, su, cv, sv = plane_tables(heading, scale, NY, nz)
        return operator, (cu, su, cv * nyquist, sv * nyquist)

    staged = held(*my_place(False))
    for contour in range(STEPS):
        by_cell = contour > 0
        if contour == 1 and CUBE:
            staged = held(*my_place(True))
        is_last = contour == STEPS - 1
        halves = lax.axis_size("dir") if is_last else 1
        moved = transport(CUBE, state, by_cell, halves, *staged, basis, damping)
        if is_last:
            moved = moved.reshape((halves, moved.shape[0] // halves) + moved.shape[1:])
            table = moment_table(orient, quad_weights)
            result = moments(moved, analysis, synthesis, decay, table)
        else:
            state = diffuse(CUBE, moved, analysis, synthesis, decay)
    return result[:, 0], jnp.moveaxis(result[:, 1:6], 1, 0)


def solution(mesh):
    in_specs = (P("dir", "shard", None, None), P(), P(), P(), P(), P(), P())
    out_specs = (P("shard", "dir"), P(None, "shard", "dir"))
    return jax.shard_map(
        on_device, mesh=mesh, in_specs=in_specs, out_specs=out_specs, check_vma=False
    )
```

```python
import functools
import math

import jax
import jax.numpy as jnp
import numpy as np
from jax import lax
from jax.experimental import pallas as pl
from jax.experimental.pallas import tpu as pltpu
from jax.sharding import PartitionSpec as P

NY = 64

transport_length = 1.5
one_third = 1.0 / 3.0
VMEM_LIMIT = 60 * 1024 * 1024
MESH = pl.DeviceIdType.MESH


def half_spectrum(ny, nz):
    selfs = [(0, 0), (ny // 2, 0), (0, nz // 2), (ny // 2, nz // 2)]
    pairs = []
    for ky in range(ny):
        for kz in range(nz):
            mirror = ((-ky) % ny, (-kz) % nz)
            if (ky, kz) < mirror:
                pairs.append((ky, kz))
    first = selfs[:2] + pairs
    second = selfs[2:] + pairs
    return np.array(first + second, np.int64)


def real_basis(ny, nz):
    freq = half_spectrum(ny, nz)
    half = len(freq) // 2
    y = np.repeat(np.arange(ny), nz)[:, None]
    z = np.tile(np.arange(nz), ny)[:, None]
    angle = 2.0 * np.pi * (y * freq[None, :, 0] / ny + z * freq[None, :, 1] / nz)
    basis = np.cos(angle)
    basis[:, half + 2 :] = -np.sin(angle[:, half + 2 :])
    return basis


def signed(k, length):
    return np.where(k <= (length - 1) // 2, k, k - length) * (2.0 * np.pi / length)


def plane_tables(heading, scale, ny, nz):
    freq = half_spectrum(ny, nz)
    lanes = len(freq)
    half = lanes // 2
    wave_y = jnp.asarray(signed(freq[:, 0], ny), jnp.float32)
    wave_z = jnp.asarray(signed(freq[:, 1], nz), jnp.float32)
    theta_y = scale * heading[1][:, None] * wave_y[None, :]
    theta_z = scale * heading[2][:, None] * wave_z[None, :]
    cy, sy, cz, sz = jnp.cos(theta_y), jnp.sin(theta_y), jnp.cos(theta_z), jnp.sin(theta_z)
    ny_mask = freq[:, 0] == ny // 2
    nz_mask = freq[:, 1] == nz // 2
    only_y = jnp.asarray(ny_mask & ~nz_mask)[None]
    only_z = jnp.asarray(nz_mask & ~ny_mask)[None]
    both = jnp.asarray(ny_mask & nz_mask)[None]
    cos_sum = cy * cz - sy * sz
    sin_sum = sy * cz + cy * sz
    single = only_y | only_z
    cu = jnp.where(single, cy * cz, cos_sum)
    su = jnp.where(only_z, sy * cz, jnp.where(only_y, sz * cy, jnp.where(both, 0.0, sin_sum)))
    cv = jnp.where(
        only_z, -cy * sz, jnp.where(only_y, -cz * sy, jnp.where(both, -sin_sum, 0.0))
    )
    sv = jnp.where(single, -sy * sz, 0.0)
    weight = np.full((lanes,), 2.0 / (ny * nz))
    weight[[0, 1, half, half + 1]] = 1.0 / (ny * nz)
    turn = np.where(np.arange(lanes) < half, 1.0, -1.0)
    weight = jnp.asarray(weight, jnp.float32)[None]
    turn = jnp.asarray(turn, jnp.float32)[None]
    return cu * weight, su * weight * turn, cv * weight, sv * weight * turn


def line_operator(heading, scale, nx, group):
    count = heading.shape[1]
    k = np.arange(1, nx // 2)
    theta = scale * heading[0][:, None] * jnp.asarray(k * (2.0 * np.pi / nx), jnp.float32)[None]
    theta_n = -scale * heading[0][:, None] * math.pi
    trig = jnp.concatenate(
        [jnp.ones((count, 1), jnp.float32), jnp.cos(theta), jnp.sin(theta), jnp.cos(theta_n)], 1
    )
    gap = (np.arange(nx)[:, None] - np.arange(nx)[None, :]) % nx
    angle = 2.0 * np.pi * ((k[:, None, None] * gap[None]) % nx) / nx
    rows = np.concatenate(
        [np.ones((1, nx, nx)), 2 * np.cos(angle), 2 * np.sin(angle), (1.0 - 2.0 * (gap % 2))[None]]
    )
    table = jnp.asarray(rows / nx, jnp.float32)
    operator = jnp.einsum("gmk,kax->gamx", trig.reshape(-1, group, nx), table,
                          precision=lax.Precision.HIGHEST)
    operator = operator.reshape(count // group, nx * group, nx)
    sign = jnp.asarray(1.0 - 2.0 * (np.arange(nx) % 2), jnp.float32)
    extra = jnp.broadcast_to(sign, (count // group, group, nx))
    operator = jnp.concatenate([operator, extra], 1).astype(jnp.bfloat16)
    return operator, jnp.sin(theta_n) / nx


def to_rows(block):
    a, b, lanes = block.shape
    if b % 16:
        return block.astype(jnp.float32).reshape(a * b, lanes).astype(jnp.bfloat16)
    return block.reshape(a * b, lanes)


def swap(values):
    half = values.shape[-1] // 2
    return jnp.concatenate([values[..., half:], values[..., :half]], axis=-1)


def greet():
    d, s = lax.axis_index("dir"), lax.axis_index("shard")
    two, n = lax.axis_size("dir"), lax.axis_size("shard")
    barrier = pltpu.get_barrier_semaphore()

    def one(k, carry):
        other = (d * n + s + k) % (two * n)
        pl.semaphore_signal(barrier, inc=1, device_id=(other // n, other % n), device_id_type=MESH)
        return carry

    lax.fori_loop(1, two * n, one, 0)


def greeted():
    others = lax.axis_size("dir") * lax.axis_size("shard") - 1
    pl.semaphore_wait(pltpu.get_barrier_semaphore(), others)


def remote(source, target, send, receive, device):
    return pltpu.make_async_remote_copy(
        src_ref=source, dst_ref=target, send_sem=send, recv_sem=receive,
        device_id=device, device_id_type=MESH,
    )


def is_me(device):
    return (device[0] == lax.axis_index("dir")) & (device[1] == lax.axis_index("shard"))


def transport(by_cell, halves, group, nx, q_ref, p_ref, tables, w_ref, damping_ref, z_ref, l_ref,
              stage_ref, ready, send):
    c_ref, s_ref, cv_ref, sv_ref = tables
    rows = nx * group
    lanes = w_ref.shape[1]
    width = lanes // halves
    groups = p_ref.shape[0]
    col = lax.broadcasted_iota(jnp.int32, (nx, rows), 1)
    line = lax.broadcasted_iota(jnp.int32, (nx, rows), 0)
    col_x = col // group if by_cell else col % nx
    expand = jnp.where(col_x == line, 1.0, 0.0).astype(jnp.bfloat16)

    chunks = 4
    part = (nx if by_cell else group) // chunks
    step_rows = rows // chunks
    part_x = nx // chunks
    first = lax.axis_index("shard") // (lax.axis_size("shard") // chunks) + chunks // 2

    def one_group(g, carry):
        wide = jnp.dot(p_ref[g], expand, preferred_element_type=jnp.float32)
        row_at = lax.broadcasted_iota(jnp.int32, wide.shape, 0)
        col_at = lax.broadcasted_iota(jnp.int32, wide.shape, 1)
        col_m = col_at % group if by_cell else col_at // nx
        l_ref[...] = jnp.where(row_at % group == col_m, wide, 0.0).astype(jnp.bfloat16)
        m_at = pl.ds(pl.multiple_of(g * group, group), group)
        if by_cell:
            ready(g)

        def forward(i, carry):
            if by_cell:
                block = to_rows(q_ref[g, pl.ds(i * part, part)])
            else:
                block = to_rows(q_ref[pl.ds(g * group + i * part, part)])
            z = jnp.dot(block, w_ref[...], preferred_element_type=jnp.float32)
            start = pl.multiple_of(i * step_rows, step_rows)
            z_ref[pl.ds(start, step_rows), :] = z.astype(jnp.bfloat16)
            return carry

        lax.fori_loop(0, chunks, forward, 0)

        ripple = jnp.dot(l_ref[rows:, :], z_ref[...], preferred_element_type=jnp.float32)
        cross = ripple * cv_ref[m_at, :] + swap(ripple) * sv_ref[m_at, :]
        if not by_cell:

            @pl.when(g == 0)
            def _():
                ready(g)

        def backward(j, carry):
            i = (first + j) % chunks
            start = pl.multiple_of(i * step_rows, step_rows)
            y = jnp.dot(l_ref[pl.ds(start, step_rows), :], z_ref[...],
                        preferred_element_type=jnp.float32)
            y = y.reshape(part_x, group, lanes)
            odd = lax.broadcasted_iota(jnp.int32, y.shape, 0) % 2 == 1
            turned = y * c_ref[m_at, :][None] + swap(y) * s_ref[m_at, :][None]
            turned = turned + jnp.where(odd, -cross[None], cross[None])
            turned = turned.reshape(step_rows, lanes).astype(jnp.bfloat16)
            back = lax.dot_general(turned, w_ref[...], (((1,), (1,)), ((), ())),
                                   preferred_element_type=jnp.float32)
            x_at = pl.ds(pl.multiple_of(i * part_x, part_x), part_x)
            back = back.reshape(part_x, group, lanes) * damping_ref[x_at, :][:, None, :]
            back = back.astype(jnp.bfloat16)
            for h in range(halves):
                stage_ref[h, g, x_at] = back[:, :, h * width : (h + 1) * width]
            send(g, i)
            return carry

        lax.fori_loop(0, chunks, backward, 0)
        return carry

    lax.fori_loop(0, groups, one_group, 0)


def loop(low, high, body):
    def step(k, carry):
        body(k)
        return carry

    lax.fori_loop(low, high, step, 0)


def chain_kernel(group, nx, q_ref, p_ref, c_ref, s_ref, cv_ref, sv_ref, w_ref, damping_ref,
                 analysis_ref, synthesis_ref, decay_ref, table_ref, out_ref, z_ref, l_ref,
                 stage1, stage2, stage3, recv1, recv2, recv3,
                 ssem1, rsem1, lsem1, ssem2, rsem2, lsem2, ssem3, rsem3, lsem3):
    greet()
    d, me = lax.axis_index("dir"), lax.axis_index("shard")
    two, n = lax.axis_size("dir"), lax.axis_size("shard")
    here = (d, me)
    groups = p_ref.shape[0]
    slab = nx // n
    parts = min(2, slab)
    some = slab // parts
    lanes = w_ref.shape[1]
    width = lanes // two
    chunks = 4
    per = n // chunks
    tables = (c_ref, s_ref, cv_ref, sv_ref)

    def to1(g, a, t):
        return stage1.at[0, g, pl.ds(t * slab + a * some, some)]

    def at1(g, a, source):
        return recv1.at[a, g, source]

    def out1(g, a, t):
        return remote(to1(g, a, t), at1(g, a, me), ssem1.at[g, a, t], rsem1.at[g, a, me], (d, t))

    def own1(g, a):
        return pltpu.make_async_copy(to1(g, a, me), at1(g, a, me), lsem1.at[g, a])

    def issue1(g, i, a):
        def one(k):
            t = i * per + (me + k) % per

            @pl.when(t == me)
            def _():
                own1(g, a).start()

            @pl.when(t != me)
            def _():
                out1(g, a, t).start()

        loop(0, per, one)

    def out2(g, i, t):
        return remote(stage2.at[g, i, t], recv2.at[g, me * slab + i], ssem2.at[g, i, t],
                      rsem2.at[g, i, me], (d, t))

    def own2(g, i):
        return pltpu.make_async_copy(stage2.at[g, i, me], recv2.at[g, me * slab + i],
                                     lsem2.at[g, i])

    def to3(g, a, h, t):
        return stage3.at[h, g, pl.ds(t * slab + a * some, some)]

    def at3(g, a, p, source):
        return recv3.at[a, p, g, source]

    def out3(g, a, h, t):
        return remote(to3(g, a, h, t), at3(g, a, d, me), ssem3.at[g, a, h * n + t],
                      rsem3.at[g, a, d * n + me], (h, t))

    def own3(g, a):
        return pltpu.make_async_copy(to3(g, a, d, me), at3(g, a, d, me), lsem3.at[g, a])

    def issue3(g, i, a):
        def one(k):
            t = i * per + (me + k) % per
            for h in range(two):
                mine = (t == me) & (d == h)

                @pl.when(mine)
                def _():
                    own3(g, a).start()

                @pl.when(jnp.logical_not(mine))
                def _():
                    out3(g, a, h, t).start()

        loop(0, per, one)

    first = me // per + chunks // 2

    def late(issue):
        for a in range(1, parts):
            loop(0, groups, lambda g: loop(0, chunks, lambda j: issue(g, (first + j) % chunks, a)))

    transport(False, 1, group, nx, q_ref, p_ref, tables, w_ref, damping_ref, z_ref, l_ref, stage1,
              lambda g: greeted(), lambda g, i: issue1(g, i, 0))
    late(issue1)

    for a in range(parts):
        def arrived1(g):
            def one(k):
                source = (me + k) % n
                remote(to1(g, a, me), at1(g, a, source), ssem1.at[g, a, me],
                       rsem1.at[g, a, source], here).wait_recv()

            loop(1, n, one)
            own1(g, a).wait()

        loop(0, groups, arrived1)

        def row1(r):
            i = a * some + r
            for j in range(2):
                at = slice(j * (lanes // 2), (j + 1) * (lanes // 2))
                block = jnp.concatenate(
                    [to_rows(recv1[a, g, :, r, :, at]) for g in range(groups)], axis=0
                )
                mixed = mix(block, analysis_ref, synthesis_ref, decay_ref)
                mixed = mixed.reshape(groups, n, group, lanes // 2).astype(jnp.bfloat16)
                for g in range(groups):
                    stage2[g, i, :, :, at] = mixed[g]

        loop(0, some, row1)

        def send2(g):
            def row(r):
                i = a * some + r
                loop(0, n // 2, lambda k: out2(g, i, (me + n // 2 + k) % n).start())
                loop(n // 2 + 1, n, lambda k: out2(g, i, (me + n // 2 + k) % n).start())
                own2(g, i).start()

            loop(0, some, row)

        loop(0, groups, send2)

    def arrived2(g):
        def row(i):
            def one(k):
                source = (me + k) % n
                remote(stage2.at[g, i, me], recv2.at[g, source * slab + i], ssem2.at[g, i, me],
                       rsem2.at[g, i, source], here).wait_recv()

            loop(1, n, one)
            own2(g, i).wait()

        loop(0, slab, row)

    transport(True, two, group, nx, recv2, p_ref, tables, w_ref, damping_ref, z_ref, l_ref, stage3,
              arrived2, lambda g, i: issue3(g, i, 0))
    late(issue3)

    for a in range(parts):
        def arrived3(g):
            def one(k):
                slot = (d * n + me + k) % (two * n)
                remote(to3(g, a, 0, me), at3(g, a, slot // n, slot % n), ssem3.at[g, a, 0],
                       rsem3.at[g, a, slot], here).wait_recv()

            loop(1, two * n, one)
            own3(g, a).wait()

        loop(0, groups, arrived3)

        def row3(r):
            product = None
            for p in range(two):
                block = jnp.concatenate(
                    [to_rows(recv3[a, p, g, :, r]) for g in range(groups)], axis=0
                )
                mixed = mix(block, analysis_ref, synthesis_ref, decay_ref)
                mixed = mixed.astype(jnp.bfloat16).astype(jnp.float32)
                product = mixed if product is None else product * mixed
            out_ref[a * some + r] = jnp.dot(table_ref[...], product,
                                            precision=lax.Precision.HIGHEST,
                                            preferred_element_type=jnp.float32)

        loop(0, some, row3)

    def sent(g):
        for a in range(parts):
            loop(1, n, lambda k: out1(g, a, (me + k) % n).wait_send())

            def one3(k):
                slot = (d * n + me + k) % (two * n)
                out3(g, a, slot // n, slot % n).wait_send()

            loop(1, two * n, one3)
        loop(0, slab, lambda i: loop(1, n, lambda k: out2(g, i, (me + k) % n).wait_send()))

    loop(0, groups, sent)


def chain(q, operator, tables, basis, damping, analysis, synthesis, decay, table):
    nx, lanes = damping.shape
    count = q.shape[0]
    group = operator.shape[1] // (nx + 1)
    rows = nx * group
    groups = count // group
    two, n = lax.axis_size("dir"), lax.axis_size("shard")
    slab = nx // n
    parts = min(2, slab)
    some = slab // parts
    width = lanes // two
    vmem = pl.BlockSpec(memory_space=pltpu.VMEM)
    half = jnp.bfloat16
    dma = pltpu.SemaphoreType.DMA
    return pl.pallas_call(
        functools.partial(chain_kernel, group, nx),
        out_shape=jax.ShapeDtypeStruct((slab, table.shape[0], width), jnp.float32),
        in_specs=[vmem] * 12,
        out_specs=vmem,
        scratch_shapes=[
            pltpu.VMEM((rows, lanes), half),
            pltpu.VMEM((rows + group, rows), half),
            pltpu.VMEM((1, groups, nx, group, lanes), half),
            pltpu.VMEM((groups, slab, n, group, lanes), half),
            pltpu.VMEM((two, groups, nx, group, width), half),
            pltpu.VMEM((parts, groups, n, some, group, lanes), half),
            pltpu.VMEM((groups, nx, group, lanes), half),
            pltpu.VMEM((parts, two, groups, n, some, group, width), half),
            dma((groups, parts, n)), dma((groups, parts, n)), dma((groups, parts)),
            dma((groups, slab, n)), dma((groups, slab, n)), dma((groups, slab)),
            dma((groups, parts, two * n)), dma((groups, parts, two * n)), dma((groups, parts)),
        ],
        compiler_params=pltpu.CompilerParams(
            vmem_limit_bytes=VMEM_LIMIT, collective_id=0, has_side_effects=True
        ),
    )(q, operator, *tables, basis, damping, analysis, synthesis, decay, table)


def mix(block, analysis_ref, synthesis_ref, decay_ref):
    harmonic = jnp.dot(analysis_ref[...], block, preferred_element_type=jnp.float32)
    harmonic = (harmonic * decay_ref[...]).astype(jnp.bfloat16)
    return jnp.dot(synthesis_ref[...], harmonic, preferred_element_type=jnp.float32)


def moment_table(orient, quad_weights):
    head_x, head_y, head_z = (orient[0], orient[1], orient[2])
    unity = jnp.ones_like(head_x)
    zero = jnp.zeros_like(head_x)
    moment_rows = [
        unity,
        head_x * head_x - one_third,
        head_y * head_y - one_third,
        head_x * head_y,
        head_x * head_z,
        head_y * head_z,
        zero,
        zero,
    ]
    return jnp.stack(moment_rows) * quad_weights[None, :]


def on_device(propagators, field, orient, quad_weights, analysis, synthesis, decay):
    state = propagators[0]
    count, nx, lanes = state.shape
    nz = lanes // NY
    group = min(16, count)
    groups = count // group
    basis = jnp.asarray(real_basis(NY, nz).astype(jnp.bfloat16))
    damping = jnp.exp(-field)
    harmonics, total = analysis.shape
    pad = -harmonics % 128

    def regroup(values, axis):
        shape = values.shape[:axis] + (-1, groups, group) + values.shape[axis + 1 :]
        values = jnp.swapaxes(values.reshape(shape), axis, axis + 1)
        return values.reshape(values.shape[:axis] + (total,) + values.shape[axis + 3 :])

    analysis = regroup(jnp.pad(analysis, ((0, pad), (0, 0))), 1)
    synthesis = regroup(jnp.pad(synthesis, ((0, 0), (0, pad))), 0)
    decay = jnp.pad(decay, (0, pad))[:, None]
    table = regroup(moment_table(orient, quad_weights), 1)
    heading = lax.dynamic_slice_in_dim(orient, lax.axis_index("shard") * count, count, 1)
    scale = (1.0 - 2.0 * lax.axis_index("dir").astype(jnp.float32)) * transport_length
    operator, nyquist = line_operator(heading, scale, nx, group)
    cu, su, cv, sv = plane_tables(heading, scale, NY, nz)
    tables = (cu, su, cv * nyquist, sv * nyquist)
    result = chain(state, operator, tables, basis, damping, analysis, synthesis, decay, table)
    return result[:, 0], jnp.moveaxis(result[:, 1:6], 1, 0)


def solution(mesh):
    in_specs = (P("dir", "shard", None, None), P(), P(), P(), P(), P(), P())
    out_specs = (P("shard", "dir"), P(None, "shard", "dir"))
    return jax.shard_map(
        on_device, mesh=mesh, in_specs=in_specs, out_specs=out_specs, check_vma=False
    )
```
